32 devices in a mesh: grp: 2 (over x), tp: 8 (over z, y), rb: 2 (over core).
Axes of the slice: x: 2, y: 2, z: 4, core: 2. Of those that a mesh axis runs over, the one named last changes fastest.
Arguments:
- peram: bfloat16 [2048, 24, 2, 1024], P(('grp', 'tp'), None, None, 'rb'), parts along dimension 0, may hold values from -1 to 1
- src_elems: bfloat16 [14, 2, 256, 256], P('grp'), parts along dimension 0, may hold values from -0.25 to 0.25
- owner_times: int32 [16, 2], P('grp'), parts along dimension 0, may hold values from 0 to 23
- diag_mom: int32 [16, 2, 2], P(('grp', 'tp')), parts along dimension 0, may hold values from 0 to 6
- diag_count: int32 [16], P(('grp', 'tp')), parts along dimension 0, may hold values from 1 to 2, as said below
Outputs:
- corr: float32 [16, 2, 2, 2], P(('grp', 'tp')), parts along dimension 0
The draws below stay inside these ranges and needn't reach their ends.
There are 2 independent parts, one for each index of `grp`. The reference program is written for one: setup_inputs(seed, part) draws one part's arguments, and reference() takes and returns one part's arrays. A program takes and returns all parts, laid end to end along the dimension named above; each array names one. Nothing has to cross between parts.
Inputs may be any that keep to these rules, and one draw needn't show every extreme that they name: `diag_count`: some pair has 2 assignments.
All inputs are finite; a program needn't handle non-finite values.
Results may differ from the reference program's by a relative error of at most 0.0031.
Values may be sent and summed in bfloat16 or wider, within the bound.
A program may use at most 128 MiB of HBM per device.

```python
import math
from functools import partial
import jax
import jax.numpy as jnp
from jax import lax

NV = 256
NSPIN = 4
NS = 1024
T_SNK = 24
NMOM = 7
MAXD = 2
PAIRS = 8


def draw_peram(key, part):
    key_base, key_col = jax.random.split(jax.random.fold_in(key, 11), 2)
    array_shape = (NS, T_SNK, 2, NS)
    column = jnp.exp(jax.random.uniform(key_col, (NS, T_SNK, 1, 1), jnp.float32) * math.log(10.0))
    noise = jax.random.truncated_normal(key_base, -4.0, 4.0, array_shape, jnp.float32)
    return (noise * column / jnp.sqrt(2.0 * NS * 21.5)).astype(jnp.bfloat16)


def draw_diag_count(key, part):
    key_val, key_pos = jax.random.split(jax.random.fold_in(key, 23))
    counts = jax.random.randint(key_val, (PAIRS,), 1, MAXD + 1, jnp.int32)
    position = jax.random.randint(key_pos, (), 0, PAIRS, jnp.int32)
    return counts.at[position].set(MAXD)


def with_ends(drawn, rng, least, high):
    longest = drawn.shape.index(max(drawn.shape))
    spots = []
    for shift in (0, 1):
        where = [jax.random.randint(jax.random.fold_in(rng, axis), (), 0, length) for axis, length in enumerate(drawn.shape)]
        where[longest] = (where[longest] + shift) % drawn.shape[longest]
        spots.append(tuple(where))
    return drawn.at[spots[0]].set(least).at[spots[1]].set(high)


def scatter_about(stream_key, shape, scale, most, kind=jnp.bfloat16):
    drawn = jax.random.normal(stream_key, shape, jnp.float32) * scale
    return jnp.minimum(jnp.maximum(drawn, -most), most).astype(kind)


def setup_inputs(seed: int = 0, part: int = 0) -> dict:
    streams_of = jax.random.split(jax.random.key(seed), 6)
    own_keys = jax.random.split(jax.random.fold_in(streams_of[5], part), 6)
    peram = draw_peram(jax.random.fold_in(jax.random.fold_in(streams_of[5], part), 71), part)
    src_elems = scatter_about(own_keys[1], (NMOM, 2, NV, NV), (2 * NV) ** -0.5, 0.25)
    owner_times = with_ends(jax.random.randint(own_keys[2], (PAIRS, 2), 0, T_SNK), jax.random.fold_in(own_keys[2], 1), 0, T_SNK - 1).astype(jnp.int32)
    diag_mom = with_ends(jax.random.randint(own_keys[3], (PAIRS, MAXD, 2), 0, NMOM), jax.random.fold_in(own_keys[3], 1), 0, NMOM - 1).astype(jnp.int32)
    diag_count = draw_diag_count(jax.random.fold_in(jax.random.fold_in(streams_of[5], part), 71), part)
    return {"peram": peram, "src_elems": src_elems, "owner_times": owner_times, "diag_mom": diag_mom, "diag_count": diag_count}


def meson_matrix(peram, time_slot):
    factor = lax.dynamic_index_in_dim(peram, time_slot, 1, keepdims=False).astype(jnp.float32)
    swapped = jnp.stack([factor[:, 1], -factor[:, 0]], axis=1)
    flat_rows = factor.reshape(NS, 2 * NS)
    flat_swap = swapped.reshape(NS, 2 * NS)
    real_part = jnp.dot(flat_rows, flat_rows.T, preferred_element_type=jnp.float32, precision=lax.Precision.HIGHEST)
    imag_part = jnp.dot(flat_rows, flat_swap.T, preferred_element_type=jnp.float32, precision=lax.Precision.HIGHEST)
    return jnp.stack([real_part, imag_part], axis=1).astype(jnp.bfloat16)


def spin_trace(element, meson):
    blocks = meson.reshape(NSPIN, NV, 2, NSPIN, NV)
    flipped = jnp.swapaxes(element, 1, 2)
    real_sum = jnp.zeros((), jnp.float32)
    imag_sum = jnp.zeros((), jnp.float32)
    for spin_index in range(NSPIN):
        diag_block = blocks[spin_index, :, :, spin_index, :]
        real_sum = real_sum + jnp.sum(flipped[0] * diag_block[:, 0] - flipped[1] * diag_block[:, 1])
        imag_sum = imag_sum + jnp.sum(flipped[0] * diag_block[:, 1] + flipped[1] * diag_block[:, 0])
    return real_sum, imag_sum


def owner_values(mesons, src_elems, owner_times, diag_mom, diag_count, owner):
    high = lax.Precision.HIGHEST
    meson_a = mesons[owner_times[owner, 0]].astype(jnp.float32)
    meson_b = mesons[owner_times[owner, 1]].astype(jnp.float32)
    rows_b = meson_b.reshape(NS, 2, NSPIN, NV)
    rows_a = meson_a.reshape(NSPIN, NV, 2, NS)
    results = []
    for slot_index in range(MAXD):
        elem_three = src_elems[diag_mom[owner, slot_index, 0]].astype(jnp.float32)
        elem_four = src_elems[diag_mom[owner, slot_index, 1]].astype(jnp.float32)
        left_re = jnp.einsum('jsl,le->jse', rows_b[:, 0], elem_four[0], precision=high) - jnp.einsum('jsl,le->jse', rows_b[:, 1], elem_four[1], precision=high)
        left_im = jnp.einsum('jsl,le->jse', rows_b[:, 0], elem_four[1], precision=high) + jnp.einsum('jsl,le->jse', rows_b[:, 1], elem_four[0], precision=high)
        right_re = jnp.einsum('le,slk->sek', elem_three[0], rows_a[:, :, 0], precision=high) + jnp.einsum('le,slk->sek', elem_three[1], rows_a[:, :, 1], precision=high)
        right_im = jnp.einsum('le,slk->sek', elem_three[1], rows_a[:, :, 0], precision=high) - jnp.einsum('le,slk->sek', elem_three[0], rows_a[:, :, 1], precision=high)
        left_re = left_re.reshape(NS, NS)
        left_im = left_im.reshape(NS, NS)
        right_re = right_re.reshape(NS, NS)
        right_im = right_im.reshape(NS, NS)
        cross_re = jnp.sum(left_re * right_re - left_im * right_im)
        cross_im = jnp.sum(left_re * right_im + left_im * right_re)
        three_re, three_im = spin_trace(elem_three, meson_a)
        four_re, four_im = spin_trace(elem_four, meson_b)
        direct_re = three_re * four_re - three_im * four_im
        direct_im = three_re * four_im + three_im * four_re
        results.append(jnp.stack([jnp.stack([direct_re, direct_im]), jnp.stack([cross_re, cross_im])]))
    stacked = 0.25 * jnp.stack(results)
    keep = (jnp.arange(MAXD, dtype=jnp.int32) < diag_count[owner])[:, None, None]
    return jnp.where(keep, stacked, jnp.zeros_like(stacked))


def reference(peram, src_elems, owner_times, diag_mom, diag_count):
    mesons = lax.map(partial(meson_matrix, peram), jnp.arange(T_SNK, dtype=jnp.int32))
    return lax.map(partial(owner_values, mesons, src_elems, owner_times, diag_mom, diag_count), jnp.arange(PAIRS, dtype=jnp.int32))
```

```python
import functools

import jax
import jax.numpy as jnp
from jax import lax
from jax.experimental import pallas as pl
from jax.experimental.pallas import tpu as pltpu
from jax.sharding import PartitionSpec as P

MESH = pl.DeviceIdType.MESH


def gather_kernel(
    owners, diags, times_ref, mom_ref, peram_ref, elems_ref, picked_ref, esel_ref,
    stage, estage, in_sem, out_sem, ein_sem, eout_sem
):
    def load(item):
        slot, owner = lax.rem(item, 2), lax.div(item, 2)
        return pltpu.make_async_copy(
            peram_ref.at[:, times_ref[owner, slot]], stage.at[slot, owner], in_sem.at[slot, owner]
        )

    def save(item):
        slot, owner = lax.rem(item, 2), lax.div(item, 2)
        return pltpu.make_async_copy(
            stage.at[slot, owner], picked_ref.at[slot, owner], out_sem.at[slot, owner]
        )

    def elem_load(item):
        return pltpu.make_async_copy(
            elems_ref.at[mom_ref[0, item // 2, item % 2]], estage.at[item], ein_sem.at[item]
        )

    def elem_save(item):
        return pltpu.make_async_copy(estage.at[item], esel_ref.at[item], eout_sem.at[item])

    def each(total, step):
        def body(item, carry):
            step(item)
            return carry

        lax.fori_loop(0, total, body, 0)

    each(2 * owners, lambda item: load(item).start())
    for item in range(2 * diags):
        elem_load(item).start()

    def forward(item):
        load(item).wait()
        save(item).start()

    each(2 * owners, forward)
    for item in range(2 * diags):
        elem_load(item).wait()
        elem_save(item).start()
    each(2 * owners, lambda item: save(item).wait())
    for item in range(2 * diags):
        elem_save(item).wait()


def dot_nt(left, right):
    return lax.dot_general(
        left, right, (((1,), (1,)), ((), ())), preferred_element_type=jnp.float32
    )


def dot_nn(left, right):
    return lax.dot_general(
        left, right, (((1,), (0,)), ((), ())), preferred_element_type=jnp.float32
    )


def fold(values):
    rows, cols = values.shape
    return jnp.sum(values.reshape(rows // 8, 8, cols), axis=0)


def main_kernel(
    n, nspin, diags, picked_ref, esel_ref, out_ref,
    recv, factor, elems, right4, left3, acc, mine, theirs,
    send_sem, recv_sem, fwd_send, fwd_recv, own_sem, own_send, own_recv, elem_sem, x_sem
):
    me = lax.axis_index("tp")
    core = lax.axis_index("rb")
    other = 1 - core
    rows, sinks = recv.shape[3], recv.shape[5]
    nv = elems.shape[-1]
    per_spin = n // nspin
    my_spin = me // per_spin
    my_place = me % per_spin

    barrier = pltpu.get_barrier_semaphore()

    def greet(step, carry):
        peer = (me + step) % n
        for target in range(2):
            pl.semaphore_signal(barrier, inc=1, device_id={"tp": peer, "rb": target}, device_id_type=MESH)
        return carry

    lax.fori_loop(1, n, greet, 0)
    pl.semaphore_signal(barrier, inc=1, device_id={"rb": other}, device_id_type=MESH)
    pl.semaphore_wait(barrier, 2 * n - 1)

    def group_at(phase):
        if nspin == 4:
            swap = my_spin + 1 - 2 * (my_spin % 2)
            far = (my_spin + 2) % 4
            last = 3 - my_spin
            return jnp.where(phase == 0, my_spin, jnp.where(phase == 1, swap, jnp.where(phase == 2, far, last)))
        return (my_spin + phase) % nspin

    def send(peer, slot):
        return pltpu.make_async_remote_copy(
            src_ref=picked_ref.at[slot, peer],
            dst_ref=recv.at[slot, me, core],
            send_sem=send_sem.at[slot, peer],
            recv_sem=recv_sem.at[me, core],
            device_id={"tp": peer, "rb": slot},
            device_id_type=MESH,
        )

    def arrival(source, half):
        return pltpu.make_async_remote_copy(
            src_ref=recv.at[core, source, half],
            dst_ref=recv.at[core, source, half],
            send_sem=send_sem.at[0, source],
            recv_sem=recv_sem.at[source, half],
            device_id={"rb": other},
            device_id_type=MESH,
        )

    def forward(slot, source, half):
        return pltpu.make_async_remote_copy(
            src_ref=recv.at[slot, source, half],
            dst_ref=recv.at[slot, source, half],
            send_sem=fwd_send.at[source, half],
            recv_sem=fwd_recv.at[source, half],
            device_id={"rb": other},
            device_id_type=MESH,
        )

    def own_local(slot):
        return pltpu.make_async_copy(picked_ref.at[slot, me], recv.at[slot, me, core], own_sem.at[slot])

    def own_remote(slot, half):
        return pltpu.make_async_remote_copy(
            src_ref=picked_ref.at[slot, me],
            dst_ref=recv.at[slot, me, half],
            send_sem=own_send.at[slot],
            recv_sem=own_recv.at[slot],
            device_id={"rb": other},
            device_id_type=MESH,
        )

    def start_phase(phase, carry):
        group = group_at(phase)

        def start_peer(step, inner):
            peer = group * per_spin + (my_place + step) % per_spin

            @pl.when(peer != me)
            def _():
                for slot in range(2):
                    send(peer, slot).start()

            return inner

        return lax.fori_loop(0, per_spin, start_peer, carry)

    lax.fori_loop(0, nspin, start_phase, 0)
    for slot in range(2):
        own_local(slot).start()
        own_remote(slot, core).start()
    elem_copy = pltpu.make_async_copy(esel_ref, elems, elem_sem)
    elem_copy.start()

    acc[...] = jnp.zeros_like(acc)
    elem_copy.wait()
    for d in range(diags):
        three_re = elems[2 * d, 0].astype(jnp.float32).T.astype(jnp.bfloat16)
        three_im = elems[2 * d, 1].astype(jnp.float32).T.astype(jnp.bfloat16)
        base = 2 * nv * d
        left3[base : base + nv, :nv] = three_re
        left3[base : base + nv, nv:] = three_im
        left3[base + nv : base + 2 * nv, :nv] = three_im
        left3[base + nv : base + 2 * nv, nv:] = -three_re
        right4[:nv, base : base + nv] = elems[2 * d + 1, 0]
        right4[:nv, base + nv : base + 2 * nv] = elems[2 * d + 1, 1]
        right4[nv:, base : base + nv] = -elems[2 * d + 1, 1]
        right4[nv:, base + nv : base + 2 * nv] = elems[2 * d + 1, 0]

    def unpack(slot, phase, source, place, half):
        planes = jnp.swapaxes(recv[slot, source, half], 0, 1)
        at = pl.ds(pl.multiple_of(place * rows, rows), rows)
        factor[slot, phase, at, half * sinks : (half + 1) * sinks] = planes[0]
        factor[slot, phase, at, (2 + half) * sinks : (3 + half) * sinks] = planes[1]

    def add_cross(product, partner):
        for d in range(diags):
            base = 2 * nv * d
            p_re, p_im = product[:, base : base + nv], product[:, base + nv : base + 2 * nv]
            q_re, q_im = partner[base : base + nv], partner[base + nv : base + 2 * nv]
            acc[6 * d] += fold(p_re * q_re - p_im * q_im)
            acc[6 * d + 1] += fold(p_re * q_im + p_im * q_re)

    def add_direct(d, which, block_re, block_im):
        e_re = elems[2 * d + which, 0].astype(jnp.float32)
        e_im = elems[2 * d + which, 1].astype(jnp.float32)
        acc[6 * d + 2 + 2 * which] += fold(e_re * block_re + e_im * block_im)
        acc[6 * d + 3 + 2 * which] += fold(e_im * block_re - e_re * block_im)

    def gram(slot, row, col):
        cut = 2 * sinks
        left, right = factor[slot, row], factor[slot, col]
        real = dot_nt(left, right)
        imag = dot_nt(left[:, :cut], right[:, cut:]) - dot_nt(left[:, cut:], right[:, :cut])
        return real.astype(jnp.bfloat16), imag.astype(jnp.bfloat16)

    def run_pair(row, col):
        a_re, a_im = gram(0, row, col)
        b_re, b_im = gram(1, row, col)
        product = dot_nn(b_re, right4[:nv]) + dot_nn(b_im, right4[nv:])
        partner = dot_nn(left3[:, :nv], a_re) + dot_nn(left3[:, nv:], a_im)
        add_cross(product, partner)
        wide = [value.astype(jnp.float32) for value in (a_re, a_im, b_re, b_im)]

        @pl.when(row != col)
        def _():
            flip_re = wide[2].T.astype(jnp.bfloat16)
            flip_im = wide[3].T.astype(jnp.bfloat16)
            product = dot_nn(flip_re, right4[:nv]) - dot_nn(flip_im, right4[nv:])
            partner = dot_nt(left3[:, :nv], a_re) - dot_nt(left3[:, nv:], a_im)
            add_cross(product, partner)

        @pl.when(row == col)
        def _():
            for d in range(diags):
                add_direct(d, 0, wide[0], wide[1])
                add_direct(d, 1, wide[2], wide[3])

    def run_phase(phase, carry):
        group = group_at(phase)

        @pl.when(phase == 0)
        def _():
            for slot in range(2):
                own_local(slot).wait()
                own_remote(slot, other).wait_recv()

        def take(place, inner):
            source = group * per_spin + place
            for half in range(2):

                @pl.when(source != me)
                def _():
                    arrival(source, half).wait_recv()
                    forward(core, source, half).start()

                unpack(core, phase, source, place, half)
            return inner

        lax.fori_loop(0, per_spin, take, 0)

        def take_forwarded(place, inner):
            source = group * per_spin + place
            for half in range(2):

                @pl.when(source != me)
                def _():
                    forward(other, source, half).wait_recv()

                unpack(other, phase, source, place, half)
            return inner

        lax.fori_loop(0, per_spin, take_forwarded, 0)

        def pair(step, inner):
            run_pair(phase, 2 * step + core)
            return inner

        return lax.fori_loop(0, (phase - core + 2) // 2, pair, carry)

    lax.fori_loop(0, nspin, run_phase, 0)

    half_lanes = nv // 2
    total = jnp.sum(acc[...], axis=1)
    mine[...] = total[:, :half_lanes] + total[:, half_lanes:]
    swap = pltpu.make_async_remote_copy(
        src_ref=mine,
        dst_ref=theirs,
        send_sem=x_sem.at[0],
        recv_sem=x_sem.at[1],
        device_id={"rb": other},
        device_id_type=MESH,
    )
    swap.start()

    def finish(step, carry):
        peer = (me + step) % n
        for slot in range(2):
            send(peer, slot).wait_send()
            forward(core, peer, slot).wait_send()
        return carry

    lax.fori_loop(1, n, finish, 0)
    for slot in range(2):
        own_remote(slot, core).wait_send()
    swap.wait()
    out_ref[...] = mine[...] + theirs[...]


def shards(peram, src_elems, owner_times, diag_mom, diag_count):
    n = lax.axis_size("tp")
    rows, _, parts, sinks = peram.shape
    nv = src_elems.shape[-1]
    nspin = n * rows // nv
    diags = diag_mom.shape[1]
    bf16, f32 = jnp.bfloat16, jnp.float32
    any_spec = pl.BlockSpec(memory_space=pl.ANY)
    smem_spec = pl.BlockSpec(memory_space=pltpu.SMEM)
    dma = pltpu.SemaphoreType.DMA
    picked, chosen = pl.pallas_call(
        functools.partial(gather_kernel, n, diags),
        out_shape=(
            jax.ShapeDtypeStruct((2, n, rows, parts, sinks), bf16),
            jax.ShapeDtypeStruct((2 * diags, 2, nv, nv), bf16),
        ),
        in_specs=[smem_spec, smem_spec, any_spec, any_spec],
        out_specs=(any_spec, any_spec),
        scratch_shapes=[
            pltpu.VMEM((2, n, rows, parts, sinks), bf16),
            pltpu.VMEM((2 * diags, 2, nv, nv), bf16),
            dma((2, n)), dma((2, n)), dma((2 * diags,)), dma((2 * diags,)),
        ],
        name="pick",
    )(owner_times, diag_mom, peram, src_elems)
    sums = 6 * diags
    lanes = nv // 2
    values = pl.pallas_call(
        functools.partial(main_kernel, n, nspin, diags),
        out_shape=jax.ShapeDtypeStruct((sums, lanes), f32),
        in_specs=[any_spec, any_spec],
        out_specs=pl.BlockSpec(memory_space=pltpu.VMEM),
        scratch_shapes=[
            pltpu.VMEM((2, n, 2, rows, parts, sinks), bf16),
            pltpu.VMEM((2, nspin, nv, 4 * sinks), bf16),
            pltpu.VMEM((2 * diags, 2, nv, nv), bf16),
            pltpu.VMEM((2 * nv, 2 * diags * nv), bf16),
            pltpu.VMEM((2 * diags * nv, 2 * nv), bf16),
            pltpu.VMEM((sums, 8, nv), f32),
            pltpu.VMEM((sums, lanes), f32),
            pltpu.VMEM((sums, lanes), f32),
            dma((2, n)), dma((n, 2)), dma((n, 2)), dma((n, 2)),
            dma((2,)), dma((2,)), dma((2,)), dma, dma((2,)),
        ],
        compiler_params=pltpu.CompilerParams(collective_id=0, has_side_effects=True),
        name="contract",
    )(picked, chosen)
    stacked = jnp.sum(values, axis=1).reshape(diags, 6)
    direct_re = stacked[:, 2] * stacked[:, 4] - stacked[:, 3] * stacked[:, 5]
    direct_im = stacked[:, 2] * stacked[:, 5] + stacked[:, 3] * stacked[:, 4]
    direct = jnp.stack([direct_re, direct_im], axis=-1)
    values_all = 0.25 * jnp.stack([direct, stacked[:, 0:2]], axis=1)
    keep = (jnp.arange(diags, dtype=jnp.int32) < diag_count[0])[:, None, None]
    return jnp.where(keep, values_all, jnp.zeros_like(values_all))[None]


def solution(mesh):
    in_specs = (
        P(("grp", "tp"), None, None, "rb"),
        P("grp", None, None, None),
        P("grp", None),
        P(("grp", "tp"), None, None),
        P(("grp", "tp")),
    )
    out_specs = P(("grp", "tp"), None, None, None)
    return jax.shard_map(shards, mesh=mesh, in_specs=in_specs, out_specs=out_specs, check_vma=False)
```

```python
import functools

import jax
import jax.numpy as jnp
from jax import lax
from jax.experimental import pallas as pl
from jax.experimental.pallas import tpu as pltpu
from jax.sharding import PartitionSpec as P

MESH = pl.DeviceIdType.MESH


def dot_nt(left, right):
    return lax.dot_general(
        left, right, (((1,), (1,)), ((), ())), preferred_element_type=jnp.float32
    )


def dot_nn(left, right):
    return lax.dot_general(
        left, right, (((1,), (0,)), ((), ())), preferred_element_type=jnp.float32
    )


def fold(values):
    rows, cols = values.shape
    return jnp.sum(values.reshape(rows // 8, 8, cols), axis=0)


def main_kernel(
    n, nspin, diags, times_hbm, mom_hbm, count_hbm, peram_ref, elems_ref, out_ref,
    slab, packed, recv, elems, right4, left3, acc, mine, theirs, times, mom, count,
    slab_sem, small_sem, elem_sem, send_sem, recv_sem, fwd_send, fwd_recv, own_send, own_recv, x_sem
):
    me = lax.axis_index("tp")
    core = lax.axis_index("rb")
    other = 1 - core
    rows, sinks = packed.shape[3], packed.shape[4]
    nv = elems.shape[-1]
    per_spin = n // nspin
    my_spin = me // per_spin
    my_place = me % per_spin

    pieces = slab_sem.shape[0]
    cut_rows = rows // pieces
    slab_copies = [
        pltpu.make_async_copy(
            peram_ref.at[pl.ds(i * cut_rows, cut_rows)], slab.at[pl.ds(i * cut_rows, cut_rows)], slab_sem.at[i]
        )
        for i in range(pieces)
    ]
    small_copies = [
        pltpu.make_async_copy(times_hbm, times, small_sem.at[0]),
        pltpu.make_async_copy(mom_hbm, mom, small_sem.at[1]),
        pltpu.make_async_copy(count_hbm, count, small_sem.at[2]),
    ]
    elem_copy = pltpu.make_async_copy(elems_ref, elems, elem_sem)
    for copy in small_copies + slab_copies:
        copy.start()
    elem_copy.start()

    barrier = pltpu.get_barrier_semaphore()

    def greet(step, carry):
        peer = (me + step) % n
        for target in range(2):
            pl.semaphore_signal(barrier, inc=1, device_id={"tp": peer, "rb": target}, device_id_type=MESH)
        return carry

    lax.fori_loop(1, n, greet, 0)
    pl.semaphore_signal(barrier, inc=1, device_id={"rb": other}, device_id_type=MESH)

    def group_at(phase):
        if nspin == 4:
            swap = my_spin + 1 - 2 * (my_spin % 2)
            far = (my_spin + 2) % 4
            last = 3 - my_spin
            return jnp.where(phase == 0, my_spin, jnp.where(phase == 1, swap, jnp.where(phase == 2, far, last)))
        return (my_spin + phase) % nspin

    def send_phase(step):
        if nspin == 4:
            inner = jnp.where(step == 0, 2, jnp.where(step == 1, 3, jnp.where(step == 2, 1, 0)))
            outer = (step + 1) % 4
            return jnp.where(((my_spin + 1) // 2) % 2 == 1, inner, outer)
        return (step + 1) % nspin

    def landing(slot, source, half):
        return recv.at[
            slot,
            :,
            pl.ds(pl.multiple_of(source * rows, rows), rows),
            pl.ds(pl.multiple_of(half * sinks, sinks), sinks),
        ]

    def send(peer, slot):
        return pltpu.make_async_remote_copy(
            src_ref=packed.at[slot, peer],
            dst_ref=landing(slot, me, core),
            send_sem=send_sem.at[slot, peer],
            recv_sem=recv_sem.at[me, core],
            device_id={"tp": peer, "rb": slot},
            device_id_type=MESH,
        )

    def arrival(source, half):
        return pltpu.make_async_remote_copy(
            src_ref=landing(core, source, half),
            dst_ref=landing(core, source, half),
            send_sem=send_sem.at[0, source],
            recv_sem=recv_sem.at[source, half],
            device_id={"rb": other},
            device_id_type=MESH,
        )

    def forward(slot, source, half):
        return pltpu.make_async_remote_copy(
            src_ref=landing(slot, source, half),
            dst_ref=landing(slot, source, half),
            send_sem=fwd_send.at[source, half],
            recv_sem=fwd_recv.at[source, half],
            device_id={"rb": other},
            device_id_type=MESH,
        )

    def own(slot, half):
        return pltpu.make_async_remote_copy(
            src_ref=landing(slot, me, half),
            dst_ref=landing(slot, me, half),
            send_sem=own_send.at[slot],
            recv_sem=own_recv.at[slot],
            device_id={"rb": other},
            device_id_type=MESH,
        )

    def peer_at(step):
        group = group_at(send_phase(step // per_spin))
        return group * per_spin + (my_place + step % per_spin) % per_spin

    for copy in small_copies + slab_copies:
        copy.wait()

    def planes_of(peer, slot):
        return jnp.swapaxes(slab[:, times[peer, slot]], 0, 1)

    def build(step):
        peer = peer_at(step)
        for slot in range(2):
            packed[slot, peer] = planes_of(peer, slot)

    def launch(step):
        peer = peer_at(step)

        @pl.when(peer != me)
        def _():
            for slot in range(2):
                send(peer, slot).start()

    build(0)
    pl.semaphore_wait(barrier, 2 * n - 1)

    def build_and_launch(step, carry):
        build(step)
        launch(step - 1)
        return carry

    lax.fori_loop(1, n, build_and_launch, 0)
    for slot in range(2):
        planes = planes_of(me, slot)
        at = pl.ds(pl.multiple_of(me * rows, rows), rows)
        recv[slot, :, at, pl.ds(pl.multiple_of(core * sinks, sinks), sinks)] = planes
    launch(n - 1)

    acc[...] = jnp.zeros_like(acc)
    elem_copy.wait()
    for d in range(diags):
        elem3, elem4 = elems[mom[0, d, 0]], elems[mom[0, d, 1]]
        three_re = elem3[0].astype(jnp.float32).T.astype(jnp.bfloat16)
        three_im = elem3[1].astype(jnp.float32).T.astype(jnp.bfloat16)
        base = 2 * nv * d
        left3[base : base + nv, :nv] = three_re
        left3[base : base + nv, nv:] = three_im
        left3[base + nv : base + 2 * nv, :nv] = three_im
        left3[base + nv : base + 2 * nv, nv:] = -three_re
        right4[:nv, base : base + nv] = elem4[0]
        right4[:nv, base + nv : base + 2 * nv] = elem4[1]
        right4[nv:, base : base + nv] = -elem4[1]
        right4[nv:, base + nv : base + 2 * nv] = elem4[0]
    for slot in range(2):
        own(slot, core).start()

    def add_cross(product, partner):
        for d in range(diags):
            base = 2 * nv * d
            p_re, p_im = product[:, base : base + nv], product[:, base + nv : base + 2 * nv]
            q_re, q_im = partner[base : base + nv], partner[base + nv : base + 2 * nv]
            acc[6 * d] += fold(p_re * q_re - p_im * q_im)
            acc[6 * d + 1] += fold(p_re * q_im + p_im * q_re)

    def add_direct(d, which, block_re, block_im):
        elem = elems[mom[0, d, which]].astype(jnp.float32)
        e_re, e_im = elem[0], elem[1]
        acc[6 * d + 2 + 2 * which] += fold(e_re * block_re + e_im * block_im)
        acc[6 * d + 3 + 2 * which] += fold(e_im * block_re - e_re * block_im)

    def gram(slot, row, col):
        def part(index, spin):
            return recv[slot, index, pl.ds(pl.multiple_of(spin * nv, nv), nv), :]

        left_re, left_im, right_re, right_im = part(0, row), part(1, row), part(0, col), part(1, col)
        real = dot_nt(left_re, right_re) + dot_nt(left_im, right_im)
        imag = dot_nt(left_re, right_im) - dot_nt(left_im, right_re)
        return real.astype(jnp.bfloat16), imag.astype(jnp.bfloat16)

    def run_pair(row, col):
        a_re, a_im = gram(0, row, col)
        b_re, b_im = gram(1, row, col)
        product = dot_nn(b_re, right4[:nv]) + dot_nn(b_im, right4[nv:])
        partner = dot_nn(left3[:, :nv], a_re) + dot_nn(left3[:, nv:], a_im)
        add_cross(product, partner)
        wide = [value.astype(jnp.float32) for value in (a_re, a_im, b_re, b_im)]

        @pl.when(row != col)
        def _():
            flip_re = wide[2].T.astype(jnp.bfloat16)
            flip_im = wide[3].T.astype(jnp.bfloat16)
            product = dot_nn(flip_re, right4[:nv]) - dot_nn(flip_im, right4[nv:])
            partner = dot_nt(left3[:, :nv], a_re) - dot_nt(left3[:, nv:], a_im)
            add_cross(product, partner)

        @pl.when(row == col)
        def _():
            for d in range(diags):
                add_direct(d, 0, wide[0], wide[1])
                add_direct(d, 1, wide[2], wide[3])

    def run_phase(phase, carry):
        group = group_at(phase)

        @pl.when(phase == 0)
        def _():
            for slot in range(2):
                own(slot, other).wait_recv()

        def source_at(step):
            return group * per_spin + (my_place + per_spin - step) % per_spin

        def take(step, inner):
            source = source_at(step)

            @pl.when(source != me)
            def _():
                for half in range(2):
                    arrival(source, half).wait_recv()
                    forward(core, source, half).start()

            return inner

        lax.fori_loop(0, per_spin, take, 0)

        def take_forwarded(step, inner):
            source = source_at(step)

            @pl.when(source != me)
            def _():
                for half in range(2):
                    forward(other, source, half).wait_recv()

            return inner

        lax.fori_loop(0, per_spin, take_forwarded, 0)

        def pair(step, inner):
            run_pair(group, group_at(2 * step + core))
            return inner

        return lax.fori_loop(0, (phase - core + 2) // 2, pair, carry)

    lax.fori_loop(0, nspin, run_phase, 0)

    half_lanes = nv // 2
    total = jnp.sum(acc[...], axis=1)
    mine[...] = total[:, :half_lanes] + total[:, half_lanes:]

    def finish(step, carry):
        peer = (me + step) % n
        for slot in range(2):
            send(peer, slot).wait_send()
            forward(core, peer, slot).wait_send()
        return carry

    lax.fori_loop(1, n, finish, 0)
    for slot in range(2):
        own(slot, core).wait_send()
    swap = pltpu.make_async_remote_copy(
        src_ref=mine,
        dst_ref=theirs,
        send_sem=x_sem.at[0],
        recv_sem=x_sem.at[1],
        device_id={"rb": other},
        device_id_type=MESH,
    )
    swap.start()
    swap.wait()
    both = mine[...] + theirs[...]
    for d in range(diags):
        c_re, c_im, t_re, t_im, f_re, f_im = (jnp.sum(both[6 * d + i : 6 * d + i + 1]) for i in range(6))
        used = d < count[0]
        line = (t_re * f_re - t_im * f_im, t_re * f_im + t_im * f_re, c_re, c_im)
        for i, value in enumerate(line):
            out_ref[4 * d + i] = jnp.where(used, 0.25 * value, 0.0)


def shards(peram, src_elems, owner_times, diag_mom, diag_count):
    n = lax.axis_size("tp")
    rows, _, parts, sinks = peram.shape
    nv = src_elems.shape[-1]
    nspin = n * rows // nv
    diags = diag_mom.shape[1]
    bf16, f32 = jnp.bfloat16, jnp.float32
    any_spec = pl.BlockSpec(memory_space=pl.ANY)
    dma = pltpu.SemaphoreType.DMA
    sums = 6 * diags
    lanes = nv // 2
    values = pl.pallas_call(
        functools.partial(main_kernel, n, nspin, diags),
        out_shape=jax.ShapeDtypeStruct((4 * diags,), f32),
        in_specs=[any_spec] * 5,
        out_specs=pl.BlockSpec(memory_space=pltpu.SMEM),
        scratch_shapes=[
            pltpu.VMEM(peram.shape, bf16),
            pltpu.VMEM((2, n, parts, rows, sinks), bf16),
            pltpu.VMEM((2, parts, n * rows, 2 * sinks), bf16),
            pltpu.VMEM(src_elems.shape, bf16),
            pltpu.VMEM((2 * nv, 2 * diags * nv), bf16),
            pltpu.VMEM((2 * diags * nv, 2 * nv), bf16),
            pltpu.VMEM((sums, 8, nv), f32),
            pltpu.VMEM((sums, lanes), f32),
            pltpu.VMEM((sums, lanes), f32),
            pltpu.SMEM(owner_times.shape, jnp.int32),
            pltpu.SMEM(diag_mom.shape, jnp.int32),
            pltpu.SMEM(diag_count.shape, jnp.int32),
            dma((4,)), dma((3,)), dma,
            dma((2, n)), dma((n, 2)), dma((n, 2)), dma((n, 2)), dma((2,)), dma((2,)), dma((2,)),
        ],
        compiler_params=pltpu.CompilerParams(collective_id=0, has_side_effects=True),
        name="contract",
    )(owner_times, diag_mom, diag_count, peram, src_elems)
    return values.reshape(1, diags, 2, 2)


def solution(mesh):
    in_specs = (
        P(("grp", "tp"), None, None, "rb"),
        P("grp", None, None, None),
        P("grp", None),
        P(("grp", "tp"), None, None),
        P(("grp", "tp")),
    )
    out_specs = P(("grp", "tp"), None, None, None)
    return jax.shard_map(shards, mesh=mesh, in_specs=in_specs, out_specs=out_specs, check_vma=False)
```

```python
import functools

import jax
import jax.numpy as jnp
from jax import lax
from jax.experimental import pallas as pl
from jax.experimental.pallas import tpu as pltpu
from jax.sharding import PartitionSpec as P

MESH = pl.DeviceIdType.MESH


def dot_nt(left, right):
    return lax.dot_general(
        left, right, (((1,), (1,)), ((), ())), preferred_element_type=jnp.float32
    )


def dot_nn(left, right):
    return lax.dot_general(
        left, right, (((1,), (0,)), ((), ())), preferred_element_type=jnp.float32
    )


def fold(values):
    rows, cols = values.shape
    return jnp.sum(values.reshape(rows // 8, 8, cols), axis=0)


def main_kernel(
    n, nspin, diags, times_hbm, mom_hbm, count_hbm, peram_ref, elems_ref, out_ref,
    slab, packed, recv, meson, elems, right4, left3, acc, mine, theirs, times, mom, count,
    slab_sem, small_sem, elem_sem, send_sem, recv_sem, fwd_send, fwd_recv, own_send, own_recv, x_sem
):
    me = lax.axis_index("tp")
    core = lax.axis_index("rb")
    other = 1 - core
    rows, sinks = packed.shape[3], packed.shape[4]
    nv = elems.shape[-1]
    subs = recv_sem.shape[2]
    sub_rows = rows // subs
    per_spin = n // nspin
    my_spin = me // per_spin
    my_place = me % per_spin
    early = per_spin // 2

    def place_at(step, sign):
        return (my_place // early + step // early) % 2 * early + (
            my_place % early + early + sign * (step % early)
        ) % early

    pieces = slab_sem.shape[0]
    cut_rows = rows // pieces
    slab_copies = [
        pltpu.make_async_copy(
            peram_ref.at[pl.ds(i * cut_rows, cut_rows)], slab.at[pl.ds(i * cut_rows, cut_rows)], slab_sem.at[i]
        )
        for i in range(pieces)
    ]
    small_copies = [
        pltpu.make_async_copy(times_hbm, times, small_sem.at[0]),
        pltpu.make_async_copy(mom_hbm, mom, small_sem.at[1]),
        pltpu.make_async_copy(count_hbm, count, small_sem.at[2]),
    ]
    elem_copy = pltpu.make_async_copy(elems_ref, elems, elem_sem)
    for copy in small_copies + slab_copies:
        copy.start()
    elem_copy.start()

    barrier = pltpu.get_barrier_semaphore()

    def greet(step, carry):
        peer = (me + step) % n
        for target in range(2):
            pl.semaphore_signal(barrier, inc=1, device_id={"tp": peer, "rb": target}, device_id_type=MESH)
        return carry

    lax.fori_loop(1, n, greet, 0)
    pl.semaphore_signal(barrier, inc=1, device_id={"rb": other}, device_id_type=MESH)

    def group_at(phase):
        if nspin == 4:
            swap = my_spin + 1 - 2 * (my_spin % 2)
            far = (my_spin + 2) % 4
            last = 3 - my_spin
            return jnp.where(phase == 0, my_spin, jnp.where(phase == 1, swap, jnp.where(phase == 2, far, last)))
        return (my_spin + phase) % nspin

    def send_phase(step):
        if nspin == 4:
            inner = jnp.where(step == 0, 2, jnp.where(step == 1, 3, jnp.where(step == 2, 1, 0)))
            outer = (step + 1) % 4
            return jnp.where(((my_spin + 1) // 2) % 2 == 1, inner, outer)
        return (step + 1) % nspin

    def landing(slot, source, half, sub):
        return recv.at[
            slot,
            :,
            pl.ds(pl.multiple_of(source * rows + sub * sub_rows, sub_rows), sub_rows),
            pl.ds(pl.multiple_of(half * sinks, sinks), sinks),
        ]

    def send(peer, slot, sub):
        return pltpu.make_async_remote_copy(
            src_ref=packed.at[slot, peer, :, pl.ds(sub * sub_rows, sub_rows)],
            dst_ref=landing(slot, me, core, sub),
            send_sem=send_sem.at[slot, peer, sub],
            recv_sem=recv_sem.at[me, core, sub],
            device_id={"tp": peer, "rb": slot},
            device_id_type=MESH,
        )

    def arrival(source, half, sub):
        return pltpu.make_async_remote_copy(
            src_ref=landing(core, source, half, sub),
            dst_ref=landing(core, source, half, sub),
            send_sem=send_sem.at[0, source, sub],
            recv_sem=recv_sem.at[source, half, sub],
            device_id={"rb": other},
            device_id_type=MESH,
        )

    def forward(slot, source, half, sub):
        return pltpu.make_async_remote_copy(
            src_ref=landing(slot, source, half, sub),
            dst_ref=landing(slot, source, half, sub),
            send_sem=fwd_send.at[source, half, sub],
            recv_sem=fwd_recv.at[source, half, sub],
            device_id={"rb": other},
            device_id_type=MESH,
        )

    def own(slot, half, sub):
        return pltpu.make_async_remote_copy(
            src_ref=landing(slot, me, half, sub),
            dst_ref=landing(slot, me, half, sub),
            send_sem=own_send.at[slot, sub],
            recv_sem=own_recv.at[slot, sub],
            device_id={"rb": other},
            device_id_type=MESH,
        )

    def peer_at(step):
        group = group_at(send_phase(step // per_spin))
        return group * per_spin + place_at(step % per_spin, 1)

    for copy in small_copies + slab_copies:
        copy.wait()

    def planes_of(peer, slot):
        return jnp.swapaxes(slab[:, times[slot, peer]], 0, 1)

    def build(step):
        peer = peer_at(step)
        for slot in range(2):
            packed[slot, peer] = planes_of(peer, slot)

    def launch(step):
        peer = peer_at(step)

        @pl.when(peer != me)
        def _():
            for slot in range(2):
                for sub in range(subs):
                    send(peer, slot, sub).start()

    build(0)
    pl.semaphore_wait(barrier, 2 * n - 1)

    def build_and_launch(step, carry):
        build(step)
        launch(step - 1)
        return carry

    lax.fori_loop(1, n, build_and_launch, 0)
    for slot in range(2):
        planes = planes_of(me, slot)
        at = pl.ds(pl.multiple_of(me * rows, rows), rows)
        recv[slot, :, at, pl.ds(pl.multiple_of(core * sinks, sinks), sinks)] = planes
    launch(n - 1)

    acc[...] = jnp.zeros_like(acc)
    elem_copy.wait()
    for d in range(diags):
        elem3, elem4 = elems[mom[0, d, 0]], elems[mom[0, d, 1]]
        three_re = elem3[0].astype(jnp.float32).T.astype(jnp.bfloat16)
        three_im = elem3[1].astype(jnp.float32).T.astype(jnp.bfloat16)
        base = 2 * nv * d
        left3[base : base + nv, :nv] = three_re
        left3[base : base + nv, nv:] = three_im
        left3[base + nv : base + 2 * nv, :nv] = three_im
        left3[base + nv : base + 2 * nv, nv:] = -three_re
        right4[:nv, base : base + nv] = elem4[0]
        right4[:nv, base + nv : base + 2 * nv] = elem4[1]
        right4[nv:, base : base + nv] = -elem4[1]
        right4[nv:, base + nv : base + 2 * nv] = elem4[0]
    for slot in range(2):
        for sub in range(subs):
            own(slot, core, sub).start()

    def add_cross(product, partner):
        for d in range(diags):
            base = 2 * nv * d
            p_re, p_im = product[:, base : base + nv], product[:, base + nv : base + 2 * nv]
            q_re, q_im = partner[base : base + nv], partner[base + nv : base + 2 * nv]
            acc[6 * d] += fold(p_re * q_re - p_im * q_im)
            acc[6 * d + 1] += fold(p_re * q_im + p_im * q_re)

    def add_direct(d, which, block_re, block_im):
        elem = elems[mom[0, d, which]].astype(jnp.float32)
        e_re, e_im = elem[0], elem[1]
        acc[6 * d + 2 + 2 * which] += fold(e_re * block_re + e_im * block_im)
        acc[6 * d + 3 + 2 * which] += fold(e_im * block_re - e_re * block_im)

    def gram(slot, step, place, start, size, col):
        def part(index, at, length):
            return recv[slot, index, pl.ds(pl.multiple_of(at, length), length), :]

        left_re, left_im = part(0, start, size), part(1, start, size)
        right_re, right_im = part(0, col * nv, nv), part(1, col * nv, nv)
        real = dot_nt(left_re, right_re) + dot_nt(left_im, right_im)
        imag = dot_nt(left_re, right_im) - dot_nt(left_im, right_re)
        to = pl.ds(pl.multiple_of(place, size), size)
        meson[slot, step, 0, to] = real.astype(jnp.bfloat16)
        meson[slot, step, 1, to] = imag.astype(jnp.bfloat16)

    def run_pair(diagonal, step, row, early_place, col):
        @pl.when(diagonal)
        def _():
            for slot in range(2):
                gram(slot, step, 0, row * nv, nv, col)

        @pl.when(jnp.logical_not(diagonal))
        def _():
            place = nv // 2 - early_place
            for slot in range(2):
                gram(slot, step, place, row * nv + place, nv // 2, col)

        a_re, a_im = meson[0, step, 0], meson[0, step, 1]
        b_re, b_im = meson[1, step, 0], meson[1, step, 1]
        product = dot_nn(b_re, right4[:nv]) + dot_nn(b_im, right4[nv:])
        partner = dot_nn(left3[:, :nv], a_re) + dot_nn(left3[:, nv:], a_im)
        add_cross(product, partner)
        wide = [value.astype(jnp.float32) for value in (a_re, a_im, b_re, b_im)]

        @pl.when(jnp.logical_not(diagonal))
        def _():
            flip_re = wide[2].T.astype(jnp.bfloat16)
            flip_im = wide[3].T.astype(jnp.bfloat16)
            product = dot_nn(flip_re, right4[:nv]) - dot_nn(flip_im, right4[nv:])
            partner = dot_nt(left3[:, :nv], a_re) - dot_nt(left3[:, nv:], a_im)
            add_cross(product, partner)

        @pl.when(diagonal)
        def _():
            for d in range(diags):
                add_direct(d, 0, wide[0], wide[1])
                add_direct(d, 1, wide[2], wide[3])

    def run_phase(phase, carry):
        group = group_at(phase)

        @pl.when(phase == 0)
        def _():
            for slot in range(2):
                for sub in range(subs):
                    own(slot, other, sub).wait_recv()

        def source_at(step):
            return group * per_spin + place_at(step, -1)

        def take(step, inner):
            source = source_at(step)

            @pl.when(source != me)
            def _():
                for sub in range(subs):
                    for half in range(2):
                        arrival(source, half, sub).wait_recv()
                        forward(core, source, half, sub).start()

            return inner

        def take_forwarded(step, inner):
            source = source_at(step)

            @pl.when(source != me)
            def _():
                for sub in range(subs):
                    for half in range(2):
                        forward(other, source, half, sub).wait_recv()

            return inner

        early_place = my_place // early * (nv // 2)
        early_at = group * nv + early_place
        lax.fori_loop(0, early, take, 0)
        lax.fori_loop(0, early, take_forwarded, 0)

        def early_rows(step, inner):
            for slot in range(2):
                gram(slot, step, early_place, early_at, nv // 2, group_at(2 * step + core))
            return inner

        lax.fori_loop(0, (phase - core + 1) // 2, early_rows, 0)
        lax.fori_loop(early, per_spin, take, 0)
        lax.fori_loop(early, per_spin, take_forwarded, 0)

        def pair(step, inner):
            run_pair(phase == 2 * step + core, step, group, early_place, group_at(2 * step + core))
            return inner

        return lax.fori_loop(0, (phase - core + 2) // 2, pair, carry)

    lax.fori_loop(0, nspin, run_phase, 0)

    half_lanes = nv // 2
    total = jnp.sum(acc[...], axis=1)
    mine[...] = total[:, :half_lanes] + total[:, half_lanes:]

    def finish(step, carry):
        peer = (me + step) % n
        for slot in range(2):
            for sub in range(subs):
                send(peer, slot, sub).wait_send()
                forward(core, peer, slot, sub).wait_send()
        return carry

    lax.fori_loop(1, n, finish, 0)
    for slot in range(2):
        for sub in range(subs):
            own(slot, core, sub).wait_send()
    swap = pltpu.make_async_remote_copy(
        src_ref=mine,
        dst_ref=theirs,
        send_sem=x_sem.at[0],
        recv_sem=x_sem.at[1],
        device_id={"rb": other},
        device_id_type=MESH,
    )
    swap.start()
    swap.wait()
    both = mine[...] + theirs[...]
    for d in range(diags):
        c_re, c_im, t_re, t_im, f_re, f_im = (jnp.sum(both[6 * d + i : 6 * d + i + 1]) for i in range(6))
        used = d < count[0]
        line = (t_re * f_re - t_im * f_im, t_re * f_im + t_im * f_re, c_re, c_im)
        for i, value in enumerate(line):
            out_ref[0, d, i // 2, i % 2] = jnp.where(used, 0.25 * value, 0.0)


def shards(peram, src_elems, owner_times, diag_mom, diag_count):
    n = lax.axis_size("tp")
    rows, _, parts, sinks = peram.shape
    nv = src_elems.shape[-1]
    nspin = n * rows // nv
    diags = diag_mom.shape[1]
    bf16, f32 = jnp.bfloat16, jnp.float32
    any_spec = pl.BlockSpec(memory_space=pl.ANY)
    dma = pltpu.SemaphoreType.DMA
    sums = 6 * diags
    subs = max(1, min(4, rows // 16 // 2))
    lanes = nv // 2
    values = pl.pallas_call(
        functools.partial(main_kernel, n, nspin, diags),
        out_shape=jax.ShapeDtypeStruct((1, diags, 2, 2), f32),
        in_specs=[any_spec] * 5,
        out_specs=pl.BlockSpec(memory_space=pltpu.SMEM),
        scratch_shapes=[
            pltpu.VMEM(peram.shape, bf16),
            pltpu.VMEM((2, n, parts, rows, sinks), bf16),
            pltpu.VMEM((2, parts, n * rows, 2 * sinks), bf16),
            pltpu.VMEM((2, nspin // 2, 2, nv, nv), bf16),
            pltpu.VMEM(src_elems.shape, bf16),
            pltpu.VMEM((2 * nv, 2 * diags * nv), bf16),
            pltpu.VMEM((2 * diags * nv, 2 * nv), bf16),
            pltpu.VMEM((sums, 8, nv), f32),
            pltpu.VMEM((sums, lanes), f32),
            pltpu.VMEM((sums, lanes), f32),
            pltpu.SMEM(owner_times.shape[::-1], jnp.int32),
            pltpu.SMEM(diag_mom.shape, jnp.int32),
            pltpu.SMEM(diag_count.shape, jnp.int32),
            dma((4,)), dma((3,)), dma,
            dma((2, n, subs)), dma((n, 2, subs)), dma((n, 2, subs)), dma((n, 2, subs)),
            dma((2, subs)), dma((2, subs)), dma((2,)),
        ],
        compiler_params=pltpu.CompilerParams(collective_id=0, has_side_effects=True),
        name="contract",
    )(owner_times.T, diag_mom, diag_count, peram, src_elems)
    return values


def solution(mesh):
    in_specs = (
        P(("grp", "tp"), None, None, "rb"),
        P("grp", None, None, None),
        P("grp", None),
        P(("grp", "tp"), None, None),
        P(("grp", "tp")),
    )
    out_specs = P(("grp", "tp"), None, None, None)
    return jax.shard_map(shards, mesh=mesh, in_specs=in_specs, out_specs=out_specs, check_vma=False)
```

```python
import functools

import jax
import jax.numpy as jnp
from jax import lax
from jax.experimental import pallas as pl
from jax.experimental.pallas import tpu as pltpu
from jax.sharding import PartitionSpec as P

MESH = pl.DeviceIdType.MESH


def dot_nt(left, right):
    return lax.dot_general(
        left, right, (((1,), (1,)), ((), ())), preferred_element_type=jnp.float32
    )


def dot_nn(left, right):
    return lax.dot_general(
        left, right, (((1,), (0,)), ((), ())), preferred_element_type=jnp.float32
    )


def fold(values):
    rows, cols = values.shape
    return jnp.sum(values.reshape(rows // 8, 8, cols), axis=0)


def main_kernel(
    n, nspin, diags, times_hbm, mom_hbm, count_hbm, peram_ref, elems_ref, out_ref,
    slab, packed, recv, meson, elems, right4, left3, acc, mine, theirs, times, mom, count,
    slab_sem, small_sem, elem_sem, send_sem, recv_sem, fwd_send, fwd_recv, own_send, own_recv, x_sem
):
    me = lax.axis_index("tp")
    core = lax.axis_index("rb")
    other = 1 - core
    rows, sinks = packed.shape[3], packed.shape[4]
    nv = elems.shape[-1]
    subs = recv_sem.shape[2]
    sub_rows = rows // subs
    per_spin = n // nspin
    my_spin = me // per_spin
    my_place = me % per_spin
    early = per_spin // 2

    def place_at(step, sign):
        return (my_place // early + step // early) % 2 * early + (
            my_place % early + early + sign * (step % early)
        ) % early

    pieces = slab_sem.shape[0]
    cut_rows = rows // pieces
    slab_copies = [
        pltpu.make_async_copy(
            peram_ref.at[pl.ds(i * cut_rows, cut_rows)], slab.at[pl.ds(i * cut_rows, cut_rows)], slab_sem.at[i]
        )
        for i in range(pieces)
    ]
    small_copies = [
        pltpu.make_async_copy(times_hbm, times, small_sem.at[0]),
        pltpu.make_async_copy(mom_hbm, mom, small_sem.at[1]),
        pltpu.make_async_copy(count_hbm, count, small_sem.at[2]),
    ]
    elem_copy = pltpu.make_async_copy(elems_ref, elems, elem_sem)
    for copy in small_copies + slab_copies:
        copy.start()
    elem_copy.start()

    barrier = pltpu.get_barrier_semaphore()

    def greet(step, carry):
        peer = (me + step) % n
        for target in range(2):
            pl.semaphore_signal(barrier, inc=1, device_id={"tp": peer, "rb": target}, device_id_type=MESH)
        return carry

    lax.fori_loop(1, n, greet, 0)
    pl.semaphore_signal(barrier, inc=1, device_id={"rb": other}, device_id_type=MESH)

    def group_at(phase):
        if nspin == 4:
            swap = my_spin + 1 - 2 * (my_spin % 2)
            far = (my_spin + 2) % 4
            last = 3 - my_spin
            return jnp.where(phase == 0, my_spin, jnp.where(phase == 1, swap, jnp.where(phase == 2, far, last)))
        return (my_spin + phase) % nspin

    def send_phase(step):
        if nspin == 4:
            inner = jnp.where(step == 0, 2, jnp.where(step == 1, 3, jnp.where(step == 2, 1, 0)))
            outer = (step + 1) % 4
            return jnp.where(((my_spin + 1) // 2) % 2 == 1, inner, outer)
        return (step + 1) % nspin

    def landing(slot, source, half, sub):
        return recv.at[
            slot,
            :,
            pl.ds(pl.multiple_of(source * rows + sub * sub_rows, sub_rows), sub_rows),
            pl.ds(pl.multiple_of(half * sinks, sinks), sinks),
        ]

    def send(peer, slot, sub):
        return pltpu.make_async_remote_copy(
            src_ref=packed.at[slot, peer, :, pl.ds(sub * sub_rows, sub_rows)],
            dst_ref=landing(slot, me, core, sub),
            send_sem=send_sem.at[slot, peer, sub],
            recv_sem=recv_sem.at[me, core, sub],
            device_id={"tp": peer, "rb": slot},
            device_id_type=MESH,
        )

    def arrival(source, half, sub):
        return pltpu.make_async_remote_copy(
            src_ref=landing(core, source, half, sub),
            dst_ref=landing(core, source, half, sub),
            send_sem=send_sem.at[0, source, sub],
            recv_sem=recv_sem.at[source, half, sub],
            device_id={"rb": other},
            device_id_type=MESH,
        )

    def forward(slot, source, half, sub):
        return pltpu.make_async_remote_copy(
            src_ref=landing(slot, source, half, sub),
            dst_ref=landing(slot, source, half, sub),
            send_sem=fwd_send.at[source, half, sub],
            recv_sem=fwd_recv.at[source, half, sub],
            device_id={"rb": other},
            device_id_type=MESH,
        )

    def own(slot, half, sub):
        return pltpu.make_async_remote_copy(
            src_ref=landing(slot, me, half, sub),
            dst_ref=landing(slot, me, half, sub),
            send_sem=own_send.at[slot, sub],
            recv_sem=own_recv.at[slot, sub],
            device_id={"rb": other},
            device_id_type=MESH,
        )

    def peer_at(step):
        group = group_at(send_phase(step // per_spin))
        return group * per_spin + place_at(step % per_spin, 1)

    for copy in small_copies + slab_copies:
        copy.wait()

    def planes_of(peer, slot):
        return jnp.swapaxes(slab[:, times[slot, peer]], 0, 1)

    def build(step):
        peer = peer_at(step)
        for slot in range(2):
            packed[slot, peer] = planes_of(peer, slot)

    def launch(step):
        peer = peer_at(step)

        @pl.when(peer != me)
        def _():
            for slot in range(2):
                for sub in range(subs):
                    send(peer, slot, sub).start()

    build(0)
    pl.semaphore_wait(barrier, 2 * n - 1)

    def build_and_launch(step, carry):
        build(step)
        launch(step - 1)
        return carry

    lax.fori_loop(1, n, build_and_launch, 0)
    for slot in range(2):
        planes = planes_of(me, slot)
        at = pl.ds(pl.multiple_of(me * rows, rows), rows)
        recv[slot, :, at, pl.ds(pl.multiple_of(core * sinks, sinks), sinks)] = planes
    launch(n - 1)

    acc[...] = jnp.zeros_like(acc)
    elem_copy.wait()
    for d in range(diags):
        elem3, elem4 = elems[mom[0, d, 0]], elems[mom[0, d, 1]]
        three_re = elem3[0].astype(jnp.float32).T.astype(jnp.bfloat16)
        three_im = elem3[1].astype(jnp.float32).T.astype(jnp.bfloat16)
        base = 2 * nv * d
        left3[base : base + nv, :nv] = three_re
        left3[base : base + nv, nv:] = three_im
        left3[base + nv : base + 2 * nv, :nv] = three_im
        left3[base + nv : base + 2 * nv, nv:] = -three_re
        right4[:nv, base : base + nv] = elem4[0]
        right4[:nv, base + nv : base + 2 * nv] = elem4[1]
        right4[nv:, base : base + nv] = -elem4[1]
        right4[nv:, base + nv : base + 2 * nv] = elem4[0]
    for slot in range(2):
        for sub in range(subs):
            own(slot, core, sub).start()

    def add_cross(product, partner):
        for d in range(diags):
            base = 2 * nv * d
            p_re, p_im = product[:, base : base + nv], product[:, base + nv : base + 2 * nv]
            q_re, q_im = partner[base : base + nv], partner[base + nv : base + 2 * nv]
            acc[6 * d] += fold(p_re * q_re - p_im * q_im)
            acc[6 * d + 1] += fold(p_re * q_im + p_im * q_re)

    def add_direct(d, which, block_re, block_im):
        elem = elems[mom[0, d, which]].astype(jnp.float32)
        e_re, e_im = elem[0], elem[1]
        acc[6 * d + 2 + 2 * which] += fold(e_re * block_re + e_im * block_im)
        acc[6 * d + 3 + 2 * which] += fold(e_im * block_re - e_re * block_im)

    def gram(slot, step, place, start, size, col):
        def part(index, at, length):
            return recv[slot, index, pl.ds(pl.multiple_of(at, length), length), :]

        left_re, left_im = part(0, start, size), part(1, start, size)
        right_re, right_im = part(0, col * nv, nv), part(1, col * nv, nv)
        real = dot_nt(left_re, right_re) + dot_nt(left_im, right_im)
        imag = dot_nt(left_re, right_im) - dot_nt(left_im, right_re)
        to = pl.ds(pl.multiple_of(place, size), size)
        meson[slot, step, 0, to] = real.astype(jnp.bfloat16)
        meson[slot, step, 1, to] = imag.astype(jnp.bfloat16)

    def run_pair(diagonal, step, row, early_place, col):
        @pl.when(diagonal)
        def _():
            for slot in range(2):
                gram(slot, step, 0, row * nv, nv, col)

        @pl.when(jnp.logical_not(diagonal))
        def _():
            place = nv // 2 - early_place
            for slot in range(2):
                gram(slot, step, place, row * nv + place, nv // 2, col)

        a_re, a_im = meson[0, step, 0], meson[0, step, 1]
        b_re, b_im = meson[1, step, 0], meson[1, step, 1]
        product = dot_nn(b_re, right4[:nv]) + dot_nn(b_im, right4[nv:])
        partner = dot_nn(left3[:, :nv], a_re) + dot_nn(left3[:, nv:], a_im)
        add_cross(product, partner)
        wide = [value.astype(jnp.float32) for value in (a_re, a_im, b_re, b_im)]

        @pl.when(jnp.logical_not(diagonal))
        def _():
            flip_re = wide[2].T.astype(jnp.bfloat16)
            flip_im = wide[3].T.astype(jnp.bfloat16)
            product = dot_nn(flip_re, right4[:nv]) - dot_nn(flip_im, right4[nv:])
            partner = dot_nt(left3[:, :nv], a_re) - dot_nt(left3[:, nv:], a_im)
            add_cross(product, partner)

        @pl.when(diagonal)
        def _():
            for d in range(diags):
                add_direct(d, 0, wide[0], wide[1])
                add_direct(d, 1, wide[2], wide[3])

    def run_phase(phase, carry):
        group = group_at(phase)

        @pl.when(phase == 0)
        def _():
            for slot in range(2):
                for sub in range(subs):
                    own(slot, other, sub).wait_recv()

        def source_at(step):
            return group * per_spin + place_at(step, -1)

        def take(step, inner):
            source = source_at(step)

            @pl.when(source != me)
            def _():
                for sub in range(subs):
                    for half in range(2):
                        arrival(source, half, sub).wait_recv()
                        forward(core, source, half, sub).start()

            return inner

        def take_forwarded(step, inner):
            source = source_at(step)

            @pl.when(source != me)
            def _():
                for sub in range(subs):
                    for half in range(2):
                        forward(other, source, half, sub).wait_recv()

            return inner

        early_place = my_place // early * (nv // 2)
        early_at = group * nv + early_place
        lax.fori_loop(0, early, take, 0)
        lax.fori_loop(0, early, take_forwarded, 0)

        def early_rows(step, inner):
            for slot in range(2):
                gram(slot, step, early_place, early_at, nv // 2, group_at(2 * step + core))
            return inner

        lax.fori_loop(0, (phase - core + 1) // 2, early_rows, 0)
        lax.fori_loop(early, per_spin, take, 0)
        lax.fori_loop(early, per_spin, take_forwarded, 0)

        def pair(step, inner):
            run_pair(phase == 2 * step + core, step, group, early_place, group_at(2 * step + core))
            return inner

        return lax.fori_loop(0, (phase - core + 2) // 2, pair, carry)

    lax.fori_loop(0, nspin, run_phase, 0)

    half_lanes = nv // 2
    total = jnp.sum(acc[...], axis=1)
    mine[...] = total[:, :half_lanes] + total[:, half_lanes:]

    def finish(step, carry):
        peer = (me + step) % n
        for slot in range(2):
            for sub in range(subs):
                send(peer, slot, sub).wait_send()
                forward(core, peer, slot, sub).wait_send()
        return carry

    lax.fori_loop(1, n, finish, 0)
    for slot in range(2):
        for sub in range(subs):
            own(slot, core, sub).wait_send()
    swap = pltpu.make_async_remote_copy(
        src_ref=mine,
        dst_ref=theirs,
        send_sem=x_sem.at[0],
        recv_sem=x_sem.at[1],
        device_id={"rb": other},
        device_id_type=MESH,
    )
    swap.start()
    swap.wait()
    both = mine[...] + theirs[...]
    for d in range(diags):
        c_re, c_im, t_re, t_im, f_re, f_im = (jnp.sum(both[6 * d + i : 6 * d + i + 1]) for i in range(6))
        used = d < count[0]
        line = (t_re * f_re - t_im * f_im, t_re * f_im + t_im * f_re, c_re, c_im)
        for i, value in enumerate(line):
            out_ref[0, d, i // 2, i % 2] = jnp.where(used, 0.25 * value, 0.0)


def shards(peram, src_elems, owner_times, diag_mom, diag_count):
    n = lax.axis_size("tp")
    rows, _, parts, sinks = peram.shape
    nv = src_elems.shape[-1]
    nspin = n * rows // nv
    diags = diag_mom.shape[1]
    bf16, f32 = jnp.bfloat16, jnp.float32
    any_spec = pl.BlockSpec(memory_space=pl.ANY)
    dma = pltpu.SemaphoreType.DMA
    sums = 6 * diags
    subs = 1
    lanes = nv // 2
    values = pl.pallas_call(
        functools.partial(main_kernel, n, nspin, diags),
        out_shape=jax.ShapeDtypeStruct((1, diags, 2, 2), f32),
        in_specs=[any_spec] * 5,
        out_specs=pl.BlockSpec(memory_space=pltpu.SMEM),
        scratch_shapes=[
            pltpu.VMEM(peram.shape, bf16),
            pltpu.VMEM((2, n, parts, rows, sinks), bf16),
            pltpu.VMEM((2, parts, n * rows, 2 * sinks), bf16),
            pltpu.VMEM((2, nspin // 2, 2, nv, nv), bf16),
            pltpu.VMEM(src_elems.shape, bf16),
            pltpu.VMEM((2 * nv, 2 * diags * nv), bf16),
            pltpu.VMEM((2 * diags * nv, 2 * nv), bf16),
            pltpu.VMEM((sums, 8, nv), f32),
            pltpu.VMEM((sums, lanes), f32),
            pltpu.VMEM((sums, lanes), f32),
            pltpu.SMEM(owner_times.shape[::-1], jnp.int32),
            pltpu.SMEM(diag_mom.shape, jnp.int32),
            pltpu.SMEM(diag_count.shape, jnp.int32),
            dma((4,)), dma((3,)), dma,
            dma((2, n, subs)), dma((n, 2, subs)), dma((n, 2, subs)), dma((n, 2, subs)),
            dma((2, subs)), dma((2, subs)), dma((2,)),
        ],
        compiler_params=pltpu.CompilerParams(collective_id=0, has_side_effects=True),
        name="contract",
    )(owner_times.T, diag_mom, diag_count, peram, src_elems)
    return values


def solution(mesh):
    in_specs = (
        P(("grp", "tp"), None, None, "rb"),
        P("grp", None, None, None),
        P("grp", None),
        P(("grp", "tp"), None, None),
        P(("grp", "tp")),
    )
    out_specs = P(("grp", "tp"), None, None, None)
    return jax.shard_map(shards, mesh=mesh, in_specs=in_specs, out_specs=out_specs, check_vma=False)
```
